256 devices in a mesh: slab: 4 (over y_hi, core), hst: 64 (over y_lo, z, x).
Axes of the slice: x: 4, y: 4 (y_hi: 2, y_lo: 2; y = y_hi * 2 + y_lo), z: 8, core: 2. Of those that a mesh axis runs over, the one named last changes fastest.
Arguments:
- load: bfloat16 [288, 524288], P('slab', 'hst'), may hold values from -6 to 6
- host_rack: int32 [524288], P('hst'), may hold values from 0 to 16383, as said below
- rack_pod: int32 [16384], P('hst'), may hold values from 0 to 127
Outputs:
- host_drift: float32 [288, 524288], P('slab', 'hst')
- rack_drift: float32 [288, 16384], P('slab', 'hst')
- pod_drift: float32 [288, 128], P('slab', 'hst')
The draws below stay inside these ranges and needn't reach their ends.
Inputs may be any that keep to these rules, and one draw needn't show every extreme that they name: `host_rack`: the hosts s * 8192 to (s + 1) * 8192 - 1 belong to racks among s * 256 to (s + 2) * 256 - 1, counted modulo 16384; racks hold uneven numbers of hosts, some none.
All inputs are finite; a program needn't handle non-finite values.
Results may differ from the reference program's by a relative error of at most 0.0003.
Values may be sent and summed in bfloat16 or wider, within the bound.
No kernel may reach another device: no remote copies, remote signals or barrier semaphores. Data moves between devices by JAX's collectives and lax.ppermute only.
A program may use at most 64 MiB of HBM per device.

```python
import math
import jax
import jax.numpy as jnp

SLAB_LEN = 36
STEPS = 288
H_DEV = 8192
R_DEV = 256
POD_DEV = 2
HOSTS = 524288
RACKS = 16384
PODS = 128


def draw_host_rack(key, part):
    shard_count = HOSTS // H_DEV
    key_rate = jax.random.fold_in(key, 11)
    key_dice = jax.random.fold_in(key, 12)
    key_first = jax.random.fold_in(key, 13)
    key_second = jax.random.fold_in(key, 14)
    host_ids = jnp.arange(HOSTS, dtype=jnp.int32)
    shard_of = host_ids // H_DEV
    local_index = host_ids % H_DEV
    spill_rate = jax.random.randint(key_rate, (shard_count,), 10, 91)
    dice_roll = jax.random.randint(key_dice, (HOSTS,), 0, 100)
    spilled = (dice_roll < spill_rate[shard_of]).astype(jnp.int32)
    first_pick = jax.random.randint(key_first, (HOSTS,), 0, R_DEV)
    second_pick = jax.random.randint(key_second, (HOSTS,), 0, R_DEV)
    within_shard = jnp.where(spilled == 1, first_pick, jnp.minimum(first_pick, second_pick))
    within_shard = jnp.where(local_index == H_DEV - 1, R_DEV - 1, within_shard)
    within_shard = jnp.where(local_index == 0, 0, within_shard)
    spilled = jnp.where((local_index == 0) | (local_index == H_DEV - 1), 0, spilled)
    return (((shard_of + spilled) * R_DEV + within_shard) % RACKS).astype(jnp.int32)


def set_ends(array, key, smallest, top_value):
    longest = array.shape.index(max(array.shape))
    spots = []
    for shift in (0, 1):
        where = [jax.random.randint(jax.random.fold_in(key, axis), (), 0, length) for axis, length in enumerate(array.shape)]
        where[longest] = (where[longest] + shift) % array.shape[longest]
        spots.append(tuple(where))
    return array.at[spots[0]].set(smallest).at[spots[1]].set(top_value)


def shard_levels(own_key, dims, pieces, low, top_value):
    level = 1.0
    for dim, parts in pieces:
        draws = jax.random.uniform(jax.random.fold_in(jax.random.fold_in(own_key, 6), dim), (parts,), jnp.float32, low / len(pieces), top_value / len(pieces))
        level = level * jnp.repeat(jnp.exp(draws), dims[dim] // parts).reshape((-1,) + (1,) * (len(dims) - 1 - dim))
    return level


def normal_values(key, shape, width, most, pieces=(), kind=jnp.bfloat16):
    gain = shard_levels(key, shape, pieces, -0.22, 0.18) if pieces else 1.0
    result = jax.random.normal(key, shape, jnp.float32) * width * gain
    return jnp.minimum(jnp.maximum(result, -most), most).astype(kind)


def setup_inputs(seed: int = 0) -> dict:
    streams_of = jax.random.split(jax.random.key(seed), 4)
    load = normal_values(streams_of[0], (STEPS, HOSTS), 1.0, 6.0, ((0, 4), (1, 64)))
    host_rack = draw_host_rack(jax.random.fold_in(streams_of[3], 71), 0)
    rack_pod = set_ends(jax.random.randint(streams_of[2], (RACKS,), 0, PODS), jax.random.fold_in(streams_of[2], 1), 0, PODS - 1).astype(jnp.int32)
    return {"load": load, "host_rack": host_rack, "rack_pod": rack_pod}


def windowed(series, half_window):
    total_steps = series.shape[0]
    extended = jnp.concatenate([series[total_steps - half_window:], series, series[:half_window]], 0)
    zero_row = jnp.zeros((1, series.shape[1]), jnp.float32)
    running = jnp.concatenate([zero_row, jnp.cumsum(extended, axis=0)], 0)
    return running[2 * half_window + 1:] - running[:total_steps]

def reference(load, host_rack, rack_pod):
    half_window = 2 * SLAB_LEN
    window_size = 2 * half_window + 1
    series = load.astype(jnp.float32)
    baseline = windowed(series, half_window) / window_size
    deviation = series - baseline
    host_sum = jnp.cumsum(deviation, axis=0)
    rack_sum = jax.ops.segment_sum(host_sum.T, host_rack, num_segments=RACKS).T
    pod_sum = jax.ops.segment_sum(rack_sum.T, rack_pod, num_segments=PODS).T
    host_drift = host_sum * (1.0 / math.sqrt(STEPS))
    rack_drift = rack_sum * (1.0 / math.sqrt(STEPS * H_DEV / R_DEV))
    pod_drift = pod_sum * (1.0 / math.sqrt(STEPS * H_DEV / POD_DEV))
    return (host_drift, rack_drift, pod_drift)
```

```python
import math

import jax
import jax.numpy as jnp
from jax import lax
from jax.sharding import Mesh, PartitionSpec as P

SLAB_LEN = 36
POD_DEV = 2
SLAB = ("y_hi", "core")
HOST = ("y_lo", "z", "x")
ROW = ("z", "x")
HIGHEST = lax.Precision.HIGHEST


def ring(value, axes, steps):
    count = lax.axis_size(axes)
    return lax.ppermute(value, axes, [(i, (i + steps) % count) for i in range(count)])


def overlap(last, low, high):
    return jnp.maximum(jnp.minimum(last, high) - jnp.maximum(low, 0) + 1, 0)


def weights(out_step, in_step, day, reach):
    seen = jnp.zeros_like(out_step + in_step)
    for turn in (-day, 0, day):
        seen += overlap(out_step, in_step + turn - reach, in_step + turn + reach)
    return jnp.where(in_step <= out_step, 2 * reach + 1, 0) - seen


def on_device(load, host_rack, rack_pod):
    rows, hosts_here = load.shape
    rack_count = rack_pod.shape[0]
    slabs = lax.axis_size(SLAB)
    shards = lax.axis_size(HOST)
    row_size = lax.axis_size(ROW)
    lines = lax.axis_size("y_lo")
    total_racks = rack_count * shards
    day = rows * slabs
    reach = 2 * SLAB_LEN
    window = 2 * reach + 1
    slab = lax.axis_index(SLAB)
    bf16, f32, i32 = jnp.bfloat16, jnp.float32, jnp.int32

    before = ring(load, SLAB, 1)
    after = ring(load, SLAB, -1)
    next_pod = ring(rack_pod, HOST, -1)

    far = (slab + slabs // 2) % slabs
    steps = lax.broadcasted_iota(i32, (1, rows), 1)
    far_weights = weights(jnp.full((1, 1), far * rows, i32), slab * rows + steps, day, reach)
    far_row = jnp.dot(far_weights.astype(bf16), load, preferred_element_type=f32)
    far_row = lax.ppermute(far_row, SLAB, [(i, (i + slabs // 2) % slabs) for i in range(slabs)])

    local_rack = (host_rack - lax.axis_index(HOST) * rack_count) % total_racks
    columns = lax.broadcasted_iota(i32, (1, 2 * rack_count), 1)
    member = (local_rack[:, None] == columns).astype(bf16)
    part = jnp.dot(load, member, preferred_element_type=f32)
    shifted = ring(part[:, rack_count:], HOST, 1)

    pod_total = POD_DEV * shards
    mine = lines * POD_DEV
    place = lax.broadcasted_iota(i32, (pod_total, 1), 0)
    pod_id = (place % mine) // POD_DEV * (row_size * POD_DEV) + place // mine * POD_DEV + place % POD_DEV
    both = jnp.concatenate([rack_pod, next_pod])
    pod_member = (pod_id == both[None, :]).astype(f32)
    pod_part = lax.dot_general(
        pod_member, part, (((1,), (1,)), ((), ())), precision=HIGHEST, preferred_element_type=f32
    )
    pod_part = lax.all_to_all(pod_part, ROW, 0, 0, tiled=True)
    pod_part = jnp.sum(pod_part.reshape(row_size, mine, rows), 0)

    racks = part[:, :rack_count] + shifted
    racks_before = ring(racks, SLAB, 1)
    racks_after = ring(racks, SLAB, -1)
    racks_far = jnp.dot(far_weights.astype(f32), racks, precision=HIGHEST)

    spare = -(-rack_count // rows)
    packed = jnp.pad(racks_far.reshape(-1), (0, spare * rows - rack_count)).reshape(spare, rows)
    sent = jnp.concatenate([pod_part, packed], 0)
    got = lax.all_gather(sent, SLAB + ("y_lo",)).reshape(slabs, lines, mine + spare, rows)
    line = lax.axis_index("y_lo")
    pods = jnp.sum(lax.dynamic_slice_in_dim(got, line * POD_DEV, POD_DEV, 2), 1)
    rack_row = lax.dynamic_index_in_dim(got, far, 0, False)
    rack_row = lax.dynamic_index_in_dim(rack_row, line, 0, False)[mine:].reshape(-1)[:rack_count]

    out_step = slab * rows + lax.broadcasted_iota(i32, (rows, 1), 0)
    near = (slab - 1) * rows + lax.broadcasted_iota(i32, (1, 3 * rows), 1)
    near_weights = weights(out_step, (near + day) % day, day, reach)
    all_weights = weights(out_step, lax.broadcasted_iota(i32, (1, day), 1), day, reach)

    near_load = jnp.concatenate([before, load, after], 0)
    host_sum = jnp.dot(near_weights.astype(bf16), near_load, preferred_element_type=f32) + far_row
    near_racks = jnp.concatenate([racks_before, racks, racks_after], 0)
    rack_sum = jnp.dot(near_weights.astype(f32), near_racks, precision=HIGHEST) + rack_row[None, :]
    pod_sum = jnp.einsum(
        "tjs,jps->pt", all_weights.astype(f32).reshape(rows, slabs, rows), pods, precision=HIGHEST
    ).T

    host_drift = host_sum * (1.0 / (window * math.sqrt(day)))
    rack_drift = rack_sum * (1.0 / (window * math.sqrt(day * hosts_here / rack_count)))
    pod_drift = pod_sum * (1.0 / (window * math.sqrt(day * hosts_here / POD_DEV)))
    return host_drift, rack_drift, pod_drift


def solution(mesh):
    slabs, shards = (mesh.shape[name] for name in ("slab", "hst"))
    devices = mesh.devices.reshape(slabs // 2, 2, 2, shards // 8, 4)
    fine = Mesh(devices, ("y_hi", "core", "y_lo", "z", "x"))
    return jax.shard_map(
        on_device,
        mesh=fine,
        in_specs=(P(SLAB, HOST), P(HOST), P(HOST)),
        out_specs=(P(SLAB, HOST),) * 3,
        check_vma=False,
    )
```

```python
import functools
import math

import jax
import jax.numpy as jnp
from jax import lax
from jax.experimental import pallas as pl
from jax.experimental.pallas import tpu as pltpu
from jax.sharding import Mesh, PartitionSpec as P

SLAB_LEN = 36
POD_DEV = 2
REACH = 2 * SLAB_LEN
WINDOW = 2 * REACH + 1
SLAB = ("y_hi", "core")
HOST = ("y_lo", "z", "x")
ROW = ("z", "x")
TILE = 8
HALF = 4
LANES = 128
BF16, F32, I32 = jnp.bfloat16, jnp.float32, jnp.int32
VMEM = pl.BlockSpec(memory_space=pltpu.VMEM)
SMEM = pl.BlockSpec(memory_space=pltpu.SMEM)
LIMIT = 62600000
NT = (((1,), (1,)), ((), ()))
NN = (((1,), (0,)), ((), ()))


def ring(value, axes, steps):
    count = lax.axis_size(axes)
    return lax.ppermute(value, axes, [(i, (i + steps) % count) for i in range(count)])


def overlap(last, low, high):
    return jnp.maximum(jnp.minimum(last, high) - jnp.maximum(low, 0) + 1, 0)


def weights(out_step, in_step, day):
    seen = jnp.zeros_like(out_step + in_step)
    for turn in (-day, 0, day):
        seen += overlap(out_step, in_step + turn - REACH, in_step + turn + REACH)
    return jnp.where(in_step <= out_step, WINDOW, 0) - seen


def thirds(value):
    high = value.astype(BF16)
    rest = value - high.astype(F32)
    middle = rest.astype(BF16)
    return high, middle, (rest - middle.astype(F32)).astype(BF16)


def exact_dot(small, value, dims):
    return sum(lax.dot_general(small, term, dims, preferred_element_type=F32) for term in thirds(value))


def rack_kernel(base_ref, slab_ref, load_ref, rack_ref, own_ref, next_ref, far_ref, *, racks, total, slabs):
    rows = load_ref.shape[0]
    slab = slab_ref[0]
    opposite = (slab + slabs // 2) % slabs

    @pl.when(pl.program_id(0) == 0)
    def _():
        own_ref[...] = jnp.zeros_like(own_ref)
        next_ref[...] = jnp.zeros_like(next_ref)

    local = rack_ref[...] - base_ref[0]
    local = jnp.where(local < 0, local + total, local)
    ahead = local >= racks
    local = jnp.where(ahead, local - racks, local)
    load = load_ref[...]
    ahead = jnp.broadcast_to(ahead.astype(F32), load.shape).astype(BF16)
    split = jnp.concatenate([load * (1 - ahead), load * ahead], 0)
    ids = lax.broadcasted_iota(I32, (racks, load.shape[1]), 0)
    member = (ids == local).astype(F32).astype(BF16)
    sums = lax.dot_general(split, member, NT, preferred_element_type=F32)
    own_ref[:rows] += sums[:rows]
    next_ref[:rows] += sums[rows:]
    day = rows * slabs
    step = lax.broadcasted_iota(I32, (rows, 1), 0)
    weight = weights(jnp.full_like(step, opposite * rows), slab * rows + step, day).astype(F32)
    far_ref[...] = jnp.sum(load.astype(F32) * weight, 0, keepdims=True)

    @pl.when(pl.program_id(0) == pl.num_programs(0) - 1)
    def _():
        for ref in (own_ref, next_ref):
            ref[rows : rows + 1] = jnp.sum(ref[:rows] * weight, 0, keepdims=True)


def total_kernel(own_ref, shifted_ref, far_ref, pod_ref, out_ref, rack_ref, sent_ref, *, per_row):
    rows, racks = rack_ref.shape
    total = own_ref[:rows] + shifted_ref[:rows]
    rack_ref[...] = total
    pod = pod_ref[...]
    shard = pod // POD_DEV
    place = shard % per_row * HALF + shard // per_row * POD_DEV + pod % POD_DEV
    count = out_ref.shape[0] * HALF
    member = (lax.broadcasted_iota(I32, (count, racks), 0) == place).astype(F32).astype(BF16)
    pods = exact_dot(member, total, NT)
    pods = jnp.concatenate([pods, jnp.zeros((count, out_ref.shape[2] - rows), F32)], 1)
    for i in range(out_ref.shape[0]):
        out_ref[i] = pods[HALF * i : HALF * (i + 1)]
    hosts = far_ref.shape[1]
    sent_ref[:, :hosts] = far_ref[...]
    sent_ref[:, hosts:] = own_ref[rows : rows + 1] + shifted_ref[rows : rows + 1]


def pack_kernel(got_ref, out_ref, *, slabs, lines):
    pods = jnp.sum(got_ref[...], 0)
    for line in range(lines):
        tile = jnp.concatenate([pods[line * POD_DEV : (line + 1) * POD_DEV], jnp.zeros((TILE - POD_DEV, LANES), F32)], 0)
        for slab in range(slabs):
            out_ref[slab * lines + line] = tile


def group_kernel(slab_ref, got_ref, cross_ref, own_ref, core_ref, far_ref, rack_ref, pod_ref, *, slabs, lines, rack_scale, pod_scale):
    rows, racks = own_ref.shape
    day = rows * slabs
    slab = slab_ref[0]
    out_step = slab * rows + lax.broadcasted_iota(I32, (rows, rows), 0)
    step = lax.broadcasted_iota(I32, (rows, rows), 1)
    core_slab = slab + 1 - 2 * (slab % 2)
    cross_slab = (slab + 2 * (slab % 2) - 1 + slabs) % slabs
    total = 0
    for other, ref in ((cross_slab, cross_ref), (slab, own_ref), (core_slab, core_ref)):
        total += exact_dot(weights(out_step, other * rows + step, day).astype(F32).astype(BF16), ref[...], NN)
    rack_ref[...] = (total + far_ref[:, far_ref.shape[1] - racks :]) * rack_scale
    pods = 0
    for other in range(slabs):
        part = sum(got_ref[other * lines + line] for line in range(lines))[:, :rows]
        matrix = weights(out_step, other * rows + step, day).astype(F32).astype(BF16)
        pods += sum(lax.dot_general(term, matrix, NT, preferred_element_type=F32) for term in thirds(part))
    pod_ref[...] = pods[:POD_DEV] * pod_scale


def call(kernel, ins, outs, name, limit=16 << 20, **more):
    return pl.pallas_call(
        kernel,
        in_specs=ins,
        out_shape=[jax.ShapeDtypeStruct(shape, F32) for shape in outs],
        compiler_params=pltpu.CompilerParams(vmem_limit_bytes=limit),
        cost_estimate=pl.CostEstimate(flops=1, bytes_accessed=1, transcendentals=0),
        name=name,
        **more,
    )


def on_device(load, host_rack, rack_pod):
    rows, hosts = load.shape
    racks = rack_pod.shape[0]
    slabs = lax.axis_size(SLAB)
    shards = lax.axis_size(HOST)
    row_size = lax.axis_size(ROW)
    lines = lax.axis_size("y_lo")
    day = rows * slabs
    slab = lax.axis_index(SLAB)
    base = lax.axis_index(HOST) * racks

    across = [(i, (i + 2 * (i % 2) - 1) % slabs) for i in range(slabs)]
    mates = [(0, 1), (1, 0)]
    cross = lax.ppermute(load, SLAB, across)

    block = 2048
    tall = rows + TILE
    own_part, next_part, far_part = call(
        functools.partial(rack_kernel, racks=racks, total=racks * shards, slabs=slabs),
        [SMEM, SMEM, pl.BlockSpec((rows, block), lambda i: (0, i)), pl.BlockSpec((1, block), lambda i: (0, i))],
        [(tall, racks), (tall, racks), (1, hosts)],
        "rack_sums",
        LIMIT,
        grid=(hosts // block,),
        out_specs=[pl.BlockSpec((tall, racks), lambda i: (0, 0))] * 2 + [pl.BlockSpec((1, block), lambda i: (0, i))],
    )(base.reshape(1), slab.reshape(1), load, host_rack.reshape(1, hosts))
    shifted = ring(next_part, HOST, 1)
    pod_part, rack_own, far_sent = call(
        functools.partial(total_kernel, per_row=row_size),
        [VMEM] * 4,
        [(row_size, HALF, LANES), (rows, racks), (1, hosts + racks)],
        "totals",
        out_specs=[VMEM] * 3,
    )(own_part, shifted, far_part, rack_pod.reshape(1, racks))

    later, pod_part, rack_own, far_sent = lax.optimization_barrier((load, pod_part, rack_own, far_sent))
    got = lax.all_to_all(pod_part, ROW, 0, 0, tiled=True)
    core = lax.ppermute(later, "core", mates)
    rack_core = lax.ppermute(rack_own, "core", mates)
    rack_cross = lax.ppermute(rack_own, SLAB, across)
    far = lax.ppermute(far_sent, SLAB, [(0, 2), (3, 1)])

    (sent,) = call(
        functools.partial(pack_kernel, slabs=slabs, lines=lines),
        [VMEM],
        [(slabs * lines, TILE, LANES)],
        "pack",
        out_specs=[VMEM],
    )(got)
    far, _ = lax.optimization_barrier((far, sent))
    got = lax.all_to_all(sent, SLAB + ("y_lo",), 0, 0, tiled=True)

    out_step = slab * rows + lax.broadcasted_iota(I32, (rows, 1), 0)
    near = lax.broadcasted_iota(I32, (1, 3 * rows), 1)
    turn = 1 - 2 * (slab % 2)
    origin = jnp.where(near < rows, slab - turn, jnp.where(near < 2 * rows, slab, slab + turn))
    near_step = (origin + slabs) % slabs * rows + near % rows
    near_weights = weights(out_step, near_step, day)
    near_load = jnp.concatenate([cross, later, core], 0)
    host_sum = jnp.dot(near_weights.astype(BF16), near_load, preferred_element_type=F32) + far[:, :hosts]
    host_drift = host_sum * (1.0 / (WINDOW * math.sqrt(day)))

    got, host_drift = lax.optimization_barrier((got, host_drift))
    rack_drift, pod_drift = call(
        functools.partial(
            group_kernel,
            slabs=slabs,
            lines=lines,
            rack_scale=1.0 / (WINDOW * math.sqrt(day * hosts / racks)),
            pod_scale=1.0 / (WINDOW * math.sqrt(day * hosts / POD_DEV)),
        ),
        [SMEM] + [VMEM] * 5,
        [(rows, racks), (POD_DEV, rows)],
        "groups",
        out_specs=[VMEM] * 2,
    )(slab.reshape(1), got, rack_cross, rack_own, rack_core, far)
    return host_drift, rack_drift, pod_drift.T


def solution(mesh):
    slabs, shards = (mesh.shape[name] for name in ("slab", "hst"))
    devices = mesh.devices.reshape(slabs // 2, 2, 2, shards // 8, 4)
    fine = Mesh(devices, ("y_hi", "core", "y_lo", "z", "x"))
    return jax.shard_map(
        on_device,
        mesh=fine,
        in_specs=(P(SLAB, HOST), P(HOST), P(HOST)),
        out_specs=(P(SLAB, HOST),) * 3,
        check_vma=False,
    )
```

```python
import functools
import math

import jax
import jax.numpy as jnp
from jax import lax
from jax.experimental import pallas as pl
from jax.experimental.pallas import tpu as pltpu
from jax.sharding import Mesh, PartitionSpec as P

SLAB_LEN = 36
POD_DEV = 2
REACH = 2 * SLAB_LEN
WINDOW = 2 * REACH + 1
SLAB = ("y_hi", "core")
HOST = ("y_lo", "z", "x")
ROW = ("z", "x")
TILE = 8
HALF = 4
LANES = 128
BF16, F32, I32 = jnp.bfloat16, jnp.float32, jnp.int32
VMEM = pl.BlockSpec(memory_space=pltpu.VMEM)
HBM = pl.BlockSpec(memory_space=pltpu.HBM)
SMEM = pl.BlockSpec(memory_space=pltpu.SMEM)
LIMIT = 62600000
NT = (((1,), (1,)), ((), ()))
NN = (((1,), (0,)), ((), ()))


def ring(value, axes, steps):
    count = lax.axis_size(axes)
    return lax.ppermute(value, axes, [(i, (i + steps) % count) for i in range(count)])


def overlap(last, low, high):
    return jnp.maximum(jnp.minimum(last, high) - jnp.maximum(low, 0) + 1, 0)


def weights(out_step, in_step, day):
    seen = jnp.zeros_like(out_step + in_step)
    for turn in (-day, 0, day):
        seen += overlap(out_step, in_step + turn - REACH, in_step + turn + REACH)
    return jnp.where(in_step <= out_step, WINDOW, 0) - seen


def thirds(value):
    high = value.astype(BF16)
    rest = value - high.astype(F32)
    middle = rest.astype(BF16)
    return high, middle, (rest - middle.astype(F32)).astype(BF16)


def exact_dot(small, value, dims):
    return sum(lax.dot_general(small, term, dims, preferred_element_type=F32) for term in thirds(value))


def rack_kernel(base_ref, slab_ref, load_ref, rack_ref, own_ref, next_ref, far_ref, *, racks, total, slabs):
    rows = load_ref.shape[0]
    slab = slab_ref[0]
    opposite = (slab + slabs // 2) % slabs

    @pl.when(pl.program_id(0) == 0)
    def _():
        own_ref[...] = jnp.zeros_like(own_ref)
        next_ref[...] = jnp.zeros_like(next_ref)

    local = rack_ref[...] - base_ref[0]
    local = jnp.where(local < 0, local + total, local)
    ahead = local >= racks
    local = jnp.where(ahead, local - racks, local)
    load = load_ref[...]
    ahead = jnp.broadcast_to(ahead.astype(F32), load.shape).astype(BF16)
    split = jnp.concatenate([load * (1 - ahead), load * ahead], 0)
    ids = lax.broadcasted_iota(I32, (racks, load.shape[1]), 0)
    member = (ids == local).astype(F32).astype(BF16)
    sums = lax.dot_general(split, member, NT, preferred_element_type=F32)
    own_ref[:rows] += sums[:rows]
    next_ref[:rows] += sums[rows:]
    day = rows * slabs
    step = lax.broadcasted_iota(I32, (rows, 1), 0)
    weight = weights(jnp.full_like(step, opposite * rows), slab * rows + step, day).astype(F32)
    far_ref[...] = jnp.sum(load.astype(F32) * weight, 0, keepdims=True)

    @pl.when(pl.program_id(0) == pl.num_programs(0) - 1)
    def _():
        for ref in (own_ref, next_ref):
            ref[rows : rows + 1] = jnp.sum(ref[:rows] * weight, 0, keepdims=True)


def total_kernel(own_ref, shifted_ref, far_ref, pod_ref, out_ref, rack_ref, sent_ref, *, per_row):
    rows, racks = rack_ref.shape
    total = own_ref[:rows] + shifted_ref[:rows]
    rack_ref[...] = total
    pod = pod_ref[...]
    shard = pod // POD_DEV
    place = shard % per_row * HALF + shard // per_row * POD_DEV + pod % POD_DEV
    count = out_ref.shape[0] * HALF
    member = (lax.broadcasted_iota(I32, (count, racks), 0) == place).astype(F32).astype(BF16)
    pods = exact_dot(member, total, NT)
    pods = jnp.concatenate([pods, jnp.zeros((count, out_ref.shape[2] - rows), F32)], 1)
    for i in range(out_ref.shape[0]):
        out_ref[i] = pods[HALF * i : HALF * (i + 1)]
    hosts = far_ref.shape[1]
    sent_ref[:, :hosts] = far_ref[...]
    sent_ref[:, hosts:] = own_ref[rows : rows + 1] + shifted_ref[rows : rows + 1]


def pack_kernel(got_ref, out_ref, *, slabs, lines):
    pods = jnp.sum(got_ref[...], 0)
    for line in range(lines):
        tile = jnp.concatenate([pods[line * POD_DEV : (line + 1) * POD_DEV], jnp.zeros((TILE - POD_DEV, LANES), F32)], 0)
        for slab in range(slabs):
            out_ref[slab * lines + line] = tile


def host_kernel(slab_ref, cross_ref, load_hbm, core_ref, far_ref, out_hbm, load_ref, out_ref, in_sems, sems, *, slabs, blocks, scale):
    rows, hosts = load_ref.shape
    width = hosts // blocks
    arrivals = []
    for i in range(blocks):
        part = pl.ds(i * width, width)
        arrivals.append(pltpu.make_async_copy(load_hbm.at[:, part], load_ref.at[:, part], in_sems.at[i]))
        arrivals[-1].start()
    day = rows * slabs
    slab = slab_ref[0]
    turn = 1 - 2 * (slab % 2)
    out_step = slab * rows + lax.broadcasted_iota(I32, (rows, rows), 0)
    step = lax.broadcasted_iota(I32, (rows, rows), 1)
    parts = [weights(out_step, (other + slabs) % slabs * rows + step, day) for other in (slab - turn, slab, slab + turn)]
    matrix = jnp.concatenate([part.astype(F32) for part in parts], 1).astype(BF16)
    copies = []
    for i in range(blocks):
        part = slice(i * width, (i + 1) * width)
        arrivals[i].wait()
        near = jnp.concatenate([ref[:, part] for ref in (cross_ref, load_ref, core_ref)], 0)
        sums = lax.dot_general(matrix, near, NN, preferred_element_type=F32)
        out_ref[:, part] = (sums + far_ref[:, part]) * scale
        part = pl.ds(i * width, width)
        copies.append(pltpu.make_async_copy(out_ref.at[:, part], out_hbm.at[:, part], sems.at[i]))
        copies[-1].start()
    for copy in copies:
        copy.wait()


def group_kernel(slab_ref, got_ref, cross_ref, own_ref, core_ref, far_ref, rack_ref, pod_ref, *, slabs, lines, rack_scale, pod_scale):
    rows, racks = own_ref.shape
    day = rows * slabs
    slab = slab_ref[0]
    out_step = slab * rows + lax.broadcasted_iota(I32, (rows, rows), 0)
    step = lax.broadcasted_iota(I32, (rows, rows), 1)
    core_slab = slab + 1 - 2 * (slab % 2)
    cross_slab = (slab + 2 * (slab % 2) - 1 + slabs) % slabs
    total = 0
    for other, ref in ((cross_slab, cross_ref), (slab, own_ref), (core_slab, core_ref)):
        total += exact_dot(weights(out_step, other * rows + step, day).astype(F32).astype(BF16), ref[...], NN)
    rack_ref[...] = (total + far_ref[:, far_ref.shape[1] - racks :]) * rack_scale
    pods = 0
    for other in range(slabs):
        part = sum(got_ref[other * lines + line] for line in range(lines))[:, :rows]
        matrix = weights(out_step, other * rows + step, day).astype(F32).astype(BF16)
        pods += sum(lax.dot_general(term, matrix, NT, preferred_element_type=F32) for term in thirds(part))
    pod_ref[...] = pods[:POD_DEV] * pod_scale


def call(kernel, ins, outs, name, limit=6 << 20, **more):
    return pl.pallas_call(
        kernel,
        in_specs=ins,
        out_shape=[jax.ShapeDtypeStruct(shape, F32) for shape in outs],
        compiler_params=pltpu.CompilerParams(vmem_limit_bytes=limit),
        cost_estimate=pl.CostEstimate(flops=1, bytes_accessed=1, transcendentals=0),
        name=name,
        **more,
    )


def on_device(load, host_rack, rack_pod):
    rows, hosts = load.shape
    racks = rack_pod.shape[0]
    slabs = lax.axis_size(SLAB)
    shards = lax.axis_size(HOST)
    row_size = lax.axis_size(ROW)
    lines = lax.axis_size("y_lo")
    day = rows * slabs
    slab = lax.axis_index(SLAB)
    base = lax.axis_index(HOST) * racks

    across = [(i, (i + 2 * (i % 2) - 1) % slabs) for i in range(slabs)]
    mates = [(0, 1), (1, 0)]
    cross = lax.ppermute(load, SLAB, across)
    core = lax.ppermute(load, "core", mates)

    blocks = 8
    block = 4096
    tall = rows + TILE
    own_part, next_part, far_part = call(
        functools.partial(rack_kernel, racks=racks, total=racks * shards, slabs=slabs),
        [SMEM, SMEM, pl.BlockSpec((rows, block), lambda i: (0, i)), pl.BlockSpec((1, block), lambda i: (0, i))],
        [(tall, racks), (tall, racks), (1, hosts)],
        "rack_sums",
        12 << 20,
        grid=(hosts // block,),
        out_specs=[pl.BlockSpec((tall, racks), lambda i: (0, 0))] * 2 + [pl.BlockSpec((1, block), lambda i: (0, i))],
    )(base.reshape(1), slab.reshape(1), *(pltpu.with_memory_space_constraint(x, pltpu.HBM) for x in (load, host_rack.reshape(1, hosts))))
    shifted = ring(next_part, HOST, 1)
    far_part, core = lax.optimization_barrier((far_part, core))
    pod_part, rack_own, far_sent = call(
        functools.partial(total_kernel, per_row=row_size),
        [VMEM] * 4,
        [(row_size, HALF, LANES), (rows, racks), (1, hosts + racks)],
        "totals",
        out_specs=[VMEM] * 3,
    )(own_part, shifted, far_part, rack_pod.reshape(1, racks))

    later, pod_part, rack_own, far_sent = lax.optimization_barrier((load, pod_part, rack_own, far_sent))
    got = lax.all_to_all(pod_part, ROW, 0, 0, tiled=True)
    rack_core = lax.ppermute(rack_own, "core", mates)
    rack_cross = lax.ppermute(rack_own, SLAB, across)
    far = lax.ppermute(far_sent, SLAB, [(0, 2), (3, 1)])

    (sent,) = call(
        functools.partial(pack_kernel, slabs=slabs, lines=lines),
        [VMEM],
        [(slabs * lines, TILE, LANES)],
        "pack",
        out_specs=[VMEM],
    )(got)
    far, _ = lax.optimization_barrier((far, sent))
    got = lax.all_to_all(sent, SLAB + ("y_lo",), 0, 0, tiled=True)

    (host_drift,) = call(
        functools.partial(host_kernel, slabs=slabs, blocks=blocks, scale=1.0 / (WINDOW * math.sqrt(day))),
        [SMEM, VMEM, HBM, VMEM, VMEM],
        [(rows, hosts)],
        "host_sums",
        out_specs=[HBM],
        scratch_shapes=[
            pltpu.VMEM((rows, hosts), BF16),
            pltpu.VMEM((rows, hosts), F32),
            pltpu.SemaphoreType.DMA((blocks,)),
            pltpu.SemaphoreType.DMA((blocks,)),
        ],
    )(slab.reshape(1), cross, pltpu.with_memory_space_constraint(load, pltpu.HBM), core, far)
    got, host_drift = lax.optimization_barrier((got, host_drift))
    rack_drift, pod_drift = call(
        functools.partial(
            group_kernel,
            slabs=slabs,
            lines=lines,
            rack_scale=1.0 / (WINDOW * math.sqrt(day * hosts / racks)),
            pod_scale=1.0 / (WINDOW * math.sqrt(day * hosts / POD_DEV)),
        ),
        [SMEM] + [VMEM] * 5,
        [(rows, racks), (POD_DEV, rows)],
        "groups",
        out_specs=[VMEM] * 2,
    )(slab.reshape(1), got, rack_cross, rack_own, rack_core, far)
    return host_drift, rack_drift, pod_drift.T


def solution(mesh):
    slabs, shards = (mesh.shape[name] for name in ("slab", "hst"))
    devices = mesh.devices.reshape(slabs // 2, 2, 2, shards // 8, 4)
    fine = Mesh(devices, ("y_hi", "core", "y_lo", "z", "x"))
    return jax.shard_map(
        on_device,
        mesh=fine,
        in_specs=(P(SLAB, HOST), P(HOST), P(HOST)),
        out_specs=(P(SLAB, HOST),) * 3,
        check_vma=False,
    )
```

```python
import functools
import math

import jax
import jax.numpy as jnp
from jax import lax
from jax.experimental import pallas as pl
from jax.experimental.pallas import tpu as pltpu
from jax.sharding import Mesh, PartitionSpec as P

SLAB_LEN = 36
POD_DEV = 2
REACH = 2 * SLAB_LEN
WINDOW = 2 * REACH + 1
SLAB = ("y_hi", "core")
HOST = ("y_lo", "z", "x")
ROW = ("z", "x")
TILE = 8
HALF = 4
LANES = 128
BF16, F32, I32 = jnp.bfloat16, jnp.float32, jnp.int32
VMEM = pl.BlockSpec(memory_space=pltpu.VMEM)
HBM = pl.BlockSpec(memory_space=pltpu.HBM)
SMEM = pl.BlockSpec(memory_space=pltpu.SMEM)
LIMIT = 62600000
NT = (((1,), (1,)), ((), ()))
NN = (((1,), (0,)), ((), ()))


def ring(value, axes, steps):
    count = lax.axis_size(axes)
    return lax.ppermute(value, axes, [(i, (i + steps) % count) for i in range(count)])


def overlap(last, low, high):
    return jnp.maximum(jnp.minimum(last, high) - jnp.maximum(low, 0) + 1, 0)


def weights(out_step, in_step, day):
    seen = jnp.zeros_like(out_step + in_step)
    for turn in (-day, 0, day):
        seen += overlap(out_step, in_step + turn - REACH, in_step + turn + REACH)
    return jnp.where(in_step <= out_step, WINDOW, 0) - seen


def thirds(value):
    high = value.astype(BF16)
    rest = value - high.astype(F32)
    middle = rest.astype(BF16)
    return high, middle, (rest - middle.astype(F32)).astype(BF16)


def exact_dot(small, value, dims):
    return sum(lax.dot_general(small, term, dims, preferred_element_type=F32) for term in thirds(value))


def rack_kernel(base_ref, slab_ref, load_ref, rack_ref, own_ref, next_ref, far_ref, *, racks, total, slabs):
    rows = load_ref.shape[0]
    slab = slab_ref[0]
    opposite = (slab + slabs // 2) % slabs

    @pl.when(pl.program_id(0) == 0)
    def _():
        own_ref[...] = jnp.zeros_like(own_ref)
        next_ref[...] = jnp.zeros_like(next_ref)

    local = rack_ref[...] - base_ref[0]
    local = jnp.where(local < 0, local + total, local)
    ahead = local >= racks
    local = jnp.where(ahead, local - racks, local)
    load = load_ref[...]
    ahead = jnp.broadcast_to(ahead.astype(F32), load.shape).astype(BF16)
    split = jnp.concatenate([load * (1 - ahead), load * ahead], 0)
    ids = lax.broadcasted_iota(I32, (racks, load.shape[1]), 0)
    member = (ids == local).astype(F32).astype(BF16)
    sums = lax.dot_general(split, member, NT, preferred_element_type=F32)
    own_ref[:rows] += sums[:rows]
    next_ref[:rows] += sums[rows:]
    day = rows * slabs
    step = lax.broadcasted_iota(I32, (rows, 1), 0)
    weight = weights(jnp.full_like(step, opposite * rows), slab * rows + step, day).astype(F32)
    far_ref[...] = jnp.sum(load.astype(F32) * weight, 0, keepdims=True)

    @pl.when(pl.program_id(0) == pl.num_programs(0) - 1)
    def _():
        for ref in (own_ref, next_ref):
            ref[rows : rows + 1] = jnp.sum(ref[:rows] * weight, 0, keepdims=True)


def total_kernel(own_ref, shifted_ref, far_ref, pod_ref, out_ref, rack_ref, sent_ref, *, per_row):
    rows, racks = rack_ref.shape
    total = own_ref[:rows] + shifted_ref[:rows]
    rack_ref[...] = total
    pod = pod_ref[...]
    shard = pod // POD_DEV
    place = shard % per_row * HALF + shard // per_row * POD_DEV + pod % POD_DEV
    count = out_ref.shape[0] * HALF
    member = (lax.broadcasted_iota(I32, (count, racks), 0) == place).astype(F32).astype(BF16)
    pods = exact_dot(member, total, NT)
    pods = jnp.concatenate([pods, jnp.zeros((count, out_ref.shape[2] - rows), F32)], 1)
    for i in range(out_ref.shape[0]):
        out_ref[i] = pods[HALF * i : HALF * (i + 1)]
    hosts = far_ref.shape[1]
    sent_ref[:, :hosts] = far_ref[...]
    sent_ref[:, hosts:] = own_ref[rows : rows + 1] + shifted_ref[rows : rows + 1]


def pack_kernel(got_ref, out_ref, *, slabs, lines):
    pods = jnp.sum(got_ref[...], 0)
    for line in range(lines):
        tile = jnp.concatenate([pods[line * POD_DEV : (line + 1) * POD_DEV], jnp.zeros((TILE - POD_DEV, LANES), F32)], 0)
        for slab in range(slabs):
            out_ref[slab * lines + line] = tile


def host_kernel(slab_ref, cross_ref, load_hbm, core_ref, far_ref, out_hbm, load_ref, out_ref, in_sems, sems, *, slabs, blocks, scale):
    rows, hosts = load_ref.shape
    width = hosts // blocks
    arrivals = []
    for i in range(blocks):
        part = pl.ds(i * width, width)
        arrivals.append(pltpu.make_async_copy(load_hbm.at[:, part], load_ref.at[:, part], in_sems.at[i]))
        arrivals[-1].start()
    day = rows * slabs
    slab = slab_ref[0]
    turn = 1 - 2 * (slab % 2)
    out_step = slab * rows + lax.broadcasted_iota(I32, (rows, rows), 0)
    step = lax.broadcasted_iota(I32, (rows, rows), 1)
    parts = [weights(out_step, (other + slabs) % slabs * rows + step, day) for other in (slab - turn, slab, slab + turn)]
    matrix = jnp.concatenate([part.astype(F32) for part in parts], 1).astype(BF16)
    copies = []
    for i in range(blocks):
        part = slice(i * width, (i + 1) * width)
        arrivals[i].wait()
        near = jnp.concatenate([ref[:, part] for ref in (cross_ref, load_ref, core_ref)], 0)
        sums = lax.dot_general(matrix, near, NN, preferred_element_type=F32)
        out_ref[:, part] = (sums + far_ref[:, part]) * scale
        part = pl.ds(i * width, width)
        copies.append(pltpu.make_async_copy(out_ref.at[:, part], out_hbm.at[:, part], sems.at[i]))
        copies[-1].start()
    for copy in copies:
        copy.wait()


def group_kernel(slab_ref, got_ref, cross_ref, own_ref, core_ref, far_ref, rack_ref, pod_ref, *, slabs, lines, rack_scale, pod_scale):
    rows, racks = own_ref.shape
    day = rows * slabs
    slab = slab_ref[0]
    out_step = slab * rows + lax.broadcasted_iota(I32, (rows, rows), 0)
    step = lax.broadcasted_iota(I32, (rows, rows), 1)
    core_slab = slab + 1 - 2 * (slab % 2)
    cross_slab = (slab + 2 * (slab % 2) - 1 + slabs) % slabs
    total = 0
    for other, ref in ((cross_slab, cross_ref), (slab, own_ref), (core_slab, core_ref)):
        total += exact_dot(weights(out_step, other * rows + step, day).astype(F32).astype(BF16), ref[...], NN)
    rack_ref[...] = (total + far_ref[:, far_ref.shape[1] - racks :]) * rack_scale
    pods = 0
    for other in range(slabs):
        part = sum(got_ref[other * lines + line] for line in range(lines))[:, :rows]
        matrix = weights(out_step, other * rows + step, day).astype(F32).astype(BF16)
        pods += sum(lax.dot_general(term, matrix, NT, preferred_element_type=F32) for term in thirds(part))
    pod_ref[...] = pods[:POD_DEV] * pod_scale


def call(kernel, ins, outs, name, limit=6 << 20, **more):
    return pl.pallas_call(
        kernel,
        in_specs=ins,
        out_shape=[jax.ShapeDtypeStruct(shape, F32) for shape in outs],
        compiler_params=pltpu.CompilerParams(vmem_limit_bytes=limit),
        cost_estimate=pl.CostEstimate(flops=1, bytes_accessed=1, transcendentals=0),
        name=name,
        **more,
    )


def on_device(load, host_rack, rack_pod):
    rows, hosts = load.shape
    racks = rack_pod.shape[0]
    slabs = lax.axis_size(SLAB)
    shards = lax.axis_size(HOST)
    row_size = lax.axis_size(ROW)
    lines = lax.axis_size("y_lo")
    day = rows * slabs
    slab = lax.axis_index(SLAB)
    base = lax.axis_index(HOST) * racks

    across = [(i, (i + 2 * (i % 2) - 1) % slabs) for i in range(slabs)]
    mates = [(0, 1), (1, 0)]
    cross = lax.ppermute(load, SLAB, across)

    blocks = 8
    block = 4096
    tall = rows + TILE
    own_part, next_part, far_part = call(
        functools.partial(rack_kernel, racks=racks, total=racks * shards, slabs=slabs),
        [SMEM, SMEM, pl.BlockSpec((rows, block), lambda i: (0, i)), pl.BlockSpec((1, block), lambda i: (0, i))],
        [(tall, racks), (tall, racks), (1, hosts)],
        "rack_sums",
        12 << 20,
        grid=(hosts // block,),
        out_specs=[pl.BlockSpec((tall, racks), lambda i: (0, 0))] * 2 + [pl.BlockSpec((1, block), lambda i: (0, i))],
    )(base.reshape(1), slab.reshape(1), *(pltpu.with_memory_space_constraint(x, pltpu.HBM) for x in (load, host_rack.reshape(1, hosts))))
    shifted = ring(next_part, HOST, 1)
    pod_part, rack_own, far_sent = call(
        functools.partial(total_kernel, per_row=row_size),
        [VMEM] * 4,
        [(row_size, HALF, LANES), (rows, racks), (1, hosts + racks)],
        "totals",
        out_specs=[VMEM] * 3,
    )(own_part, shifted, far_part, rack_pod.reshape(1, racks))

    later, pod_part, rack_own, far_sent = lax.optimization_barrier((load, pod_part, rack_own, far_sent))
    got = lax.all_to_all(pod_part, ROW, 0, 0, tiled=True)
    core = lax.ppermute(later, "core", mates)
    rack_core = lax.ppermute(rack_own, "core", mates)
    rack_cross = lax.ppermute(rack_own, SLAB, across)
    far = lax.ppermute(far_sent, SLAB, [(0, 2), (3, 1)])

    (sent,) = call(
        functools.partial(pack_kernel, slabs=slabs, lines=lines),
        [VMEM],
        [(slabs * lines, TILE, LANES)],
        "pack",
        out_specs=[VMEM],
    )(got)
    far, _ = lax.optimization_barrier((far, sent))
    got = lax.all_to_all(sent, SLAB + ("y_lo",), 0, 0, tiled=True)

    (host_drift,) = call(
        functools.partial(host_kernel, slabs=slabs, blocks=blocks, scale=1.0 / (WINDOW * math.sqrt(day))),
        [SMEM, VMEM, HBM, VMEM, VMEM],
        [(rows, hosts)],
        "host_sums",
        out_specs=[HBM],
        scratch_shapes=[
            pltpu.VMEM((rows, hosts), BF16),
            pltpu.VMEM((rows, hosts), F32),
            pltpu.SemaphoreType.DMA((blocks,)),
            pltpu.SemaphoreType.DMA((blocks,)),
        ],
    )(slab.reshape(1), cross, pltpu.with_memory_space_constraint(load, pltpu.HBM), core, far)
    got, host_drift = lax.optimization_barrier((got, host_drift))
    rack_drift, pod_drift = call(
        functools.partial(
            group_kernel,
            slabs=slabs,
            lines=lines,
            rack_scale=1.0 / (WINDOW * math.sqrt(day * hosts / racks)),
            pod_scale=1.0 / (WINDOW * math.sqrt(day * hosts / POD_DEV)),
        ),
        [SMEM] + [VMEM] * 5,
        [(rows, racks), (POD_DEV, rows)],
        "groups",
        out_specs=[VMEM] * 2,
    )(slab.reshape(1), got, rack_cross, rack_own, rack_core, far)
    return host_drift, rack_drift, pod_drift.T


def solution(mesh):
    slabs, shards = (mesh.shape[name] for name in ("slab", "hst"))
    devices = mesh.devices.reshape(slabs // 2, 2, 2, shards // 8, 4)
    fine = Mesh(devices, ("y_hi", "core", "y_lo", "z", "x"))
    return jax.shard_map(
        on_device,
        mesh=fine,
        in_specs=(P(SLAB, HOST), P(HOST), P(HOST)),
        out_specs=(P(SLAB, HOST),) * 3,
        check_vma=False,
    )
```

```python
import functools
import math

import jax
import jax.numpy as jnp
from jax import lax
from jax.experimental import pallas as pl
from jax.experimental.pallas import tpu as pltpu
from jax.sharding import Mesh, PartitionSpec as P

SLAB_LEN = 36
POD_DEV = 2
REACH = 2 * SLAB_LEN
WINDOW = 2 * REACH + 1
SLAB = ("y_hi", "core")
HOST = ("y_lo", "z", "x")
ROW = ("z", "x")
TILE = 8
HALF = 4
LANES = 128
BF16, F32, I32 = jnp.bfloat16, jnp.float32, jnp.int32
VMEM = pl.BlockSpec(memory_space=pltpu.VMEM)
HBM = pl.BlockSpec(memory_space=pltpu.HBM)
SMEM = pl.BlockSpec(memory_space=pltpu.SMEM)
LIMIT = 62600000
NT = (((1,), (1,)), ((), ()))
NN = (((1,), (0,)), ((), ()))


def ring(value, axes, steps):
    count = lax.axis_size(axes)
    return lax.ppermute(value, axes, [(i, (i + steps) % count) for i in range(count)])


def overlap(last, low, high):
    return jnp.maximum(jnp.minimum(last, high) - jnp.maximum(low, 0) + 1, 0)


def weights(out_step, in_step, day):
    seen = jnp.zeros_like(out_step + in_step)
    for turn in (-day, 0, day):
        seen += overlap(out_step, in_step + turn - REACH, in_step + turn + REACH)
    return jnp.where(in_step <= out_step, WINDOW, 0) - seen


def thirds(value):
    high = value.astype(BF16)
    rest = value - high.astype(F32)
    middle = rest.astype(BF16)
    return high, middle, (rest - middle.astype(F32)).astype(BF16)


def exact_dot(small, value, dims):
    return sum(lax.dot_general(small, term, dims, preferred_element_type=F32) for term in thirds(value))


def rack_kernel(base_ref, slab_ref, load_ref, rack_ref, own_ref, next_ref, far_ref, *, racks, total, slabs):
    rows = load_ref.shape[0]
    slab = slab_ref[0]
    opposite = (slab + slabs // 2) % slabs

    @pl.when(pl.program_id(0) == 0)
    def _():
        own_ref[...] = jnp.zeros_like(own_ref)
        next_ref[...] = jnp.zeros_like(next_ref)

    local = rack_ref[...] - base_ref[0]
    local = jnp.where(local < 0, local + total, local)
    ahead = local >= racks
    local = jnp.where(ahead, local - racks, local)
    load = load_ref[...]
    ahead = jnp.broadcast_to(ahead.astype(F32), load.shape).astype(BF16)
    split = jnp.concatenate([load * (1 - ahead), load * ahead], 0)
    ids = lax.broadcasted_iota(I32, (racks, load.shape[1]), 0)
    member = (ids == local).astype(F32).astype(BF16)
    sums = lax.dot_general(split, member, NT, preferred_element_type=F32)
    own_ref[:rows] += sums[:rows]
    next_ref[:rows] += sums[rows:]
    day = rows * slabs
    step = lax.broadcasted_iota(I32, (rows, 1), 0)
    weight = weights(jnp.full_like(step, opposite * rows), slab * rows + step, day).astype(F32)
    far_ref[...] = jnp.sum(load.astype(F32) * weight, 0, keepdims=True)

    @pl.when(pl.program_id(0) == pl.num_programs(0) - 1)
    def _():
        for ref in (own_ref, next_ref):
            ref[rows : rows + 1] = jnp.sum(ref[:rows] * weight, 0, keepdims=True)


def total_kernel(own_ref, shifted_ref, far_ref, pod_ref, out_ref, rack_ref, sent_ref, *, per_row):
    rows, racks = rack_ref.shape
    total = own_ref[:rows] + shifted_ref[:rows]
    rack_ref[...] = total
    pod = pod_ref[...]
    shard = pod // POD_DEV
    place = shard % per_row * HALF + shard // per_row * POD_DEV + pod % POD_DEV
    count = out_ref.shape[0] * HALF
    member = (lax.broadcasted_iota(I32, (count, racks), 0) == place).astype(F32).astype(BF16)
    pods = exact_dot(member, total, NT)
    pods = jnp.concatenate([pods, jnp.zeros((count, out_ref.shape[2] - rows), F32)], 1)
    for i in range(out_ref.shape[0]):
        out_ref[i] = pods[HALF * i : HALF * (i + 1)]
    hosts = far_ref.shape[1]
    sent_ref[:, :hosts] = far_ref[...]
    sent_ref[:, hosts:] = own_ref[rows : rows + 1] + shifted_ref[rows : rows + 1]


def pack_kernel(got_ref, out_ref, *, slabs, lines):
    pods = jnp.sum(got_ref[...], 0)
    for line in range(lines):
        tile = jnp.concatenate([pods[line * POD_DEV : (line + 1) * POD_DEV], jnp.zeros((TILE - POD_DEV, LANES), F32)], 0)
        for slab in range(slabs):
            out_ref[slab * lines + line] = tile


def host_weights(slab, rows, slabs, turns):
    out_step = slab * rows + lax.broadcasted_iota(I32, (rows, rows), 0)
    step = lax.broadcasted_iota(I32, (rows, rows), 1)
    parts = [weights(out_step, (slab + turn + slabs) % slabs * rows + step, rows * slabs) for turn in turns]
    return jnp.concatenate([part.astype(F32) for part in parts], 1).astype(BF16)


def chip_kernel(slab_ref, load_hbm, core_ref, sum_ref, load_ref, sems, *, slabs, blocks):
    rows, hosts = load_ref.shape
    width = hosts // blocks
    arrivals = []
    for i in range(blocks):
        part = pl.ds(i * width, width)
        arrivals.append(pltpu.make_async_copy(load_hbm.at[:, part], load_ref.at[:, part], sems.at[i]))
        arrivals[-1].start()
    slab = slab_ref[0]
    matrix = host_weights(slab, rows, slabs, (0, 1 - 2 * (slab % 2)))
    for i in range(blocks):
        part = slice(i * width, (i + 1) * width)
        arrivals[i].wait()
        near = jnp.concatenate([load_ref[:, part], core_ref[:, part]], 0)
        sum_ref[:, part] = lax.dot_general(matrix, near, NN, preferred_element_type=F32)


def host_kernel(slab_ref, cross_ref, sum_ref, far_ref, out_hbm, out_ref, sems, *, slabs, blocks, scale):
    rows, hosts = sum_ref.shape
    width = hosts // blocks
    slab = slab_ref[0]
    matrix = host_weights(slab, rows, slabs, (2 * (slab % 2) - 1,))
    copies = []
    for i in range(blocks):
        part = slice(i * width, (i + 1) * width)
        sums = lax.dot_general(matrix, cross_ref[:, part], NN, preferred_element_type=F32)
        out_ref[:, part] = (sums + sum_ref[:, part] + far_ref[:, part]) * scale
        part = pl.ds(i * width, width)
        copies.append(pltpu.make_async_copy(out_ref.at[:, part], out_hbm.at[:, part], sems.at[i]))
        copies[-1].start()
    for copy in copies:
        copy.wait()


def group_kernel(slab_ref, got_ref, cross_ref, own_ref, core_ref, far_ref, rack_ref, pod_ref, *, slabs, lines, rack_scale, pod_scale):
    rows, racks = own_ref.shape
    day = rows * slabs
    slab = slab_ref[0]
    out_step = slab * rows + lax.broadcasted_iota(I32, (rows, rows), 0)
    step = lax.broadcasted_iota(I32, (rows, rows), 1)
    core_slab = slab + 1 - 2 * (slab % 2)
    cross_slab = (slab + 2 * (slab % 2) - 1 + slabs) % slabs
    total = 0
    for other, ref in ((cross_slab, cross_ref), (slab, own_ref), (core_slab, core_ref)):
        total += exact_dot(weights(out_step, other * rows + step, day).astype(F32).astype(BF16), ref[...], NN)
    rack_ref[...] = (total + far_ref[:, far_ref.shape[1] - racks :]) * rack_scale
    pods = 0
    for other in range(slabs):
        part = sum(got_ref[other * lines + line] for line in range(lines))[:, :rows]
        matrix = weights(out_step, other * rows + step, day).astype(F32).astype(BF16)
        pods += sum(lax.dot_general(term, matrix, NT, preferred_element_type=F32) for term in thirds(part))
    pod_ref[...] = pods[:POD_DEV] * pod_scale


def call(kernel, ins, outs, name, limit=6 << 20, **more):
    return pl.pallas_call(
        kernel,
        in_specs=ins,
        out_shape=[jax.ShapeDtypeStruct(shape, F32) for shape in outs],
        compiler_params=pltpu.CompilerParams(vmem_limit_bytes=limit),
        cost_estimate=pl.CostEstimate(flops=1, bytes_accessed=1, transcendentals=0),
        name=name,
        **more,
    )


def on_device(load, host_rack, rack_pod):
    rows, hosts = load.shape
    racks = rack_pod.shape[0]
    slabs = lax.axis_size(SLAB)
    shards = lax.axis_size(HOST)
    row_size = lax.axis_size(ROW)
    lines = lax.axis_size("y_lo")
    day = rows * slabs
    slab = lax.axis_index(SLAB)
    base = lax.axis_index(HOST) * racks

    across = [(i, (i + 2 * (i % 2) - 1) % slabs) for i in range(slabs)]
    mates = [(0, 1), (1, 0)]
    cross = lax.ppermute(load, SLAB, across)
    core = lax.ppermute(load, "core", mates)

    blocks = 8
    block = 4096
    tall = rows + TILE
    own_part, next_part, far_part = call(
        functools.partial(rack_kernel, racks=racks, total=racks * shards, slabs=slabs),
        [SMEM, SMEM, pl.BlockSpec((rows, block), lambda i: (0, i)), pl.BlockSpec((1, block), lambda i: (0, i))],
        [(tall, racks), (tall, racks), (1, hosts)],
        "rack_sums",
        12 << 20,
        grid=(hosts // block,),
        out_specs=[pl.BlockSpec((tall, racks), lambda i: (0, 0))] * 2 + [pl.BlockSpec((1, block), lambda i: (0, i))],
    )(base.reshape(1), slab.reshape(1), *(pltpu.with_memory_space_constraint(x, pltpu.HBM) for x in (load, host_rack.reshape(1, hosts))))
    shifted = ring(next_part, HOST, 1)
    far_part, core = lax.optimization_barrier((far_part, core))
    pod_part, rack_own, far_sent = call(
        functools.partial(total_kernel, per_row=row_size),
        [VMEM] * 4,
        [(row_size, HALF, LANES), (rows, racks), (1, hosts + racks)],
        "totals",
        out_specs=[VMEM] * 3,
    )(own_part, shifted, far_part, rack_pod.reshape(1, racks))

    later, pod_part, rack_own, far_sent = lax.optimization_barrier((load, pod_part, rack_own, far_sent))
    got = lax.all_to_all(pod_part, ROW, 0, 0, tiled=True)
    rack_core = lax.ppermute(rack_own, "core", mates)
    rack_cross = lax.ppermute(rack_own, SLAB, across)
    far = lax.ppermute(far_sent, SLAB, [(0, 2), (3, 1)])

    (chip_sum,) = call(
        functools.partial(chip_kernel, slabs=slabs, blocks=blocks),
        [SMEM, HBM, VMEM],
        [(rows, hosts)],
        "chip_sums",
        out_specs=[VMEM],
        scratch_shapes=[pltpu.VMEM((rows, hosts), BF16), pltpu.SemaphoreType.DMA((blocks,))],
    )(slab.reshape(1), pltpu.with_memory_space_constraint(load, pltpu.HBM), core)
    (sent,) = call(
        functools.partial(pack_kernel, slabs=slabs, lines=lines),
        [VMEM],
        [(slabs * lines, TILE, LANES)],
        "pack",
        out_specs=[VMEM],
    )(got)
    far, _ = lax.optimization_barrier((far, sent))
    got = lax.all_to_all(sent, SLAB + ("y_lo",), 0, 0, tiled=True)

    (host_drift,) = call(
        functools.partial(host_kernel, slabs=slabs, blocks=blocks, scale=1.0 / (WINDOW * math.sqrt(day))),
        [SMEM] + [VMEM] * 3,
        [(rows, hosts)],
        "host_sums",
        out_specs=[HBM],
        scratch_shapes=[pltpu.VMEM((rows, hosts), F32), pltpu.SemaphoreType.DMA((blocks,))],
    )(slab.reshape(1), cross, chip_sum, far)

    got, host_drift = lax.optimization_barrier((got, host_drift))
    rack_drift, pod_drift = call(
        functools.partial(
            group_kernel,
            slabs=slabs,
            lines=lines,
            rack_scale=1.0 / (WINDOW * math.sqrt(day * hosts / racks)),
            pod_scale=1.0 / (WINDOW * math.sqrt(day * hosts / POD_DEV)),
        ),
        [SMEM] + [VMEM] * 5,
        [(rows, racks), (POD_DEV, rows)],
        "groups",
        out_specs=[VMEM] * 2,
    )(slab.reshape(1), got, rack_cross, rack_own, rack_core, far)
    return host_drift, rack_drift, pod_drift.T


def solution(mesh):
    slabs, shards = (mesh.shape[name] for name in ("slab", "hst"))
    devices = mesh.devices.reshape(slabs // 2, 2, 2, shards // 8, 4)
    fine = Mesh(devices, ("y_hi", "core", "y_lo", "z", "x"))
    return jax.shard_map(
        on_device,
        mesh=fine,
        in_specs=(P(SLAB, HOST), P(HOST), P(HOST)),
        out_specs=(P(SLAB, HOST),) * 3,
        check_vma=False,
    )
```
